32 devices in a mesh: grp: 2 (over x), tile: 8 (over z, y), wave: 2 (over core).
Axes of the slice: x: 2, y: 2, z: 4, core: 2. Of those that a mesh axis runs over, the one named last changes fastest.
Arguments:
- residual: float32 [16, 8, 2, 8, 128], P(('grp', 'tile'), 'wave'), parts along dimension 0, may hold values from -210 to 210
- kernel: bfloat16 [16, 8, 9, 2, 128, 128], P(('grp', 'tile'), 'wave'), parts along dimension 0, may hold values from -0.125 to 0.125
- offsets: float32 [16, 8, 2, 128], P(('grp', 'tile'), 'wave'), parts along dimension 0, may hold values from 0 to 1
- neighbor: int32 [16, 8, 9], P(('grp', 'tile'), 'wave'), parts along dimension 0, may hold values from 0 to 8, each once within a row
- frequency: int32 [16], P('grp'), parts along dimension 0, may hold values from 0 to 7, each once
- lattice_x: int32 [128], replicated, may hold values from 0 to 127, each once
- lattice_y: int32 [128], replicated, may hold values from 0 to 127, each once
- spectral_weight: float32 [8, 128, 128], replicated, may hold values from 0.1 to 3
Outputs:
- image_two: float32 [16, 8, 2, 8, 128], P(('grp', 'tile'), 'wave'), parts along dimension 0
- arnoldi: float32 [8, 8], P('grp'), parts along dimension 0
The draws below stay inside these ranges and needn't reach their ends.
There are 2 independent parts, one for each index of `grp`. The reference program is written for one: setup_inputs(seed, part) draws one part's arguments, and reference() takes and returns one part's arrays. A program takes and returns all parts, laid end to end along the dimension named above; an argument that names none is the same for every part. Nothing has to cross between parts.
Inputs may be any that keep to these rules, and one draw needn't show every extreme that they name: `neighbor`: each row names each of the nine neighbour slots once. `frequency`: each index appears once. `lattice_x`: each index appears once. `lattice_y`: each index appears once.
All inputs are finite; a program needn't handle non-finite values.
Results may differ from the reference program's by a relative error of at most 0.013.
Values may be sent and summed in bfloat16 or wider, within the bound.
A program may use at most 64 MiB of HBM per device.

```python
import math
import jax
import jax.numpy as jnp
from jax import lax

PANELS_T = 128
VECTORS = 8
MODES_X = 128
MODES_Y = 128
FREQUENCIES = 8
GRID_X = 8
GRID_Y = 8
PANELS = 8192


def draw_residual(key, part):
    key_a, key_b = jax.random.split(key, 2)
    full_shape = (GRID_X, GRID_Y, 2, VECTORS, PANELS_T)
    column = jnp.arange(GRID_X, dtype=jnp.float32)[:, None, None, None, None] / max(GRID_X - 1, 1)
    spread = 10.0 ** jax.random.uniform(key_b, (GRID_X, GRID_Y, 1, 1, PANELS_T), dtype=jnp.float32)
    rising = 3.0 ** column
    values = jnp.clip(jax.random.normal(key_a, full_shape, dtype=jnp.float32), -4.0, 4.0)
    return values * rising * spread


def level_of(key, shape, cuts, least, top_value):
    gain = 1.0
    for dim, parts in cuts:
        heights = jax.random.uniform(jax.random.fold_in(jax.random.fold_in(key, 6), dim), (parts,), jnp.float32, least / len(cuts), top_value / len(cuts))
        gain = gain * jnp.repeat(jnp.exp(heights), shape[dim] // parts).reshape((-1,) + (1,) * (len(shape) - 1 - dim))
    return gain


def gaussian(own_key, shape, scale, most, cuts=(), kind=jnp.bfloat16):
    gain = level_of(own_key, shape, cuts, -0.22, 0.18) if cuts else 1.0
    entries = jax.random.normal(own_key, shape, jnp.float32) * scale * gain
    return jnp.minimum(jnp.maximum(entries, -most), most).astype(kind)


def setup_inputs(seed: int = 0, part: int = 0) -> dict:
    key_list = jax.random.split(jax.random.key(seed), 9)
    part_keys = jax.random.split(jax.random.fold_in(key_list[8], part), 9)
    return {
        "residual": draw_residual(jax.random.fold_in(jax.random.fold_in(key_list[8], part), 71), part),
        "kernel": gaussian(part_keys[1], (GRID_X, GRID_Y, 9, 2, PANELS_T, PANELS_T), (18 * PANELS_T) ** -0.5, 0.125, ((0, 8), (1, 2))),
        "offsets": jnp.clip(1.0 * jax.random.uniform(part_keys[2], (GRID_X, GRID_Y, 2, PANELS_T), jnp.float32) ** level_of(part_keys[2], (GRID_X, GRID_Y, 2, PANELS_T), ((0, 8), (1, 2)), -0.2, 0.2), 0.0, 1.0),
        "neighbor": jax.vmap(lambda own: jax.random.permutation(own, 9))(jax.random.split(part_keys[3], GRID_X * GRID_Y)).reshape((GRID_X, GRID_Y, 9)).astype(jnp.int32),
        "frequency": jax.random.permutation(part_keys[4], FREQUENCIES).astype(jnp.int32),
        "lattice_x": jax.random.permutation(key_list[5], MODES_X).astype(jnp.int32),
        "lattice_y": jax.random.permutation(key_list[6], MODES_Y).astype(jnp.int32),
        "spectral_weight": jnp.clip(jnp.exp(jax.random.uniform(key_list[7], (FREQUENCIES, MODES_X, MODES_Y), jnp.float32, math.log(0.1), math.log(3.0))), 0.1, 3.0),
    }


two_pi = 2.0 * math.pi
eps_norm = 1e-06

def phase_table(position, harmonic):
    phase_angle = two_pi * (position[:, None] * harmonic[None, :])
    return (jnp.cos(phase_angle).astype(jnp.bfloat16), jnp.sin(phase_angle).astype(jnp.bfloat16))

def project_rows(cosine_cols, sine_cols, twisted):
    row_count = cosine_cols.shape[1]
    stacked = jnp.concatenate([cosine_cols, sine_cols], 1)
    gram_matrix = lax.dot_general(stacked, twisted, (((0,), (0,)), ((), ())), preferred_element_type=jnp.float32)
    gram_matrix = gram_matrix.reshape(2, row_count, 2, -1)
    coef_real = gram_matrix[0, :, 0] + gram_matrix[1, :, 1]
    coef_imag = gram_matrix[0, :, 1] - gram_matrix[1, :, 0]
    return jnp.stack([coef_real, coef_imag], 1)

def expand_rows(cosine_cols, sine_cols, scaled):
    row_count = scaled.shape[0]
    upper_rows = scaled.reshape(row_count, -1)
    lower_rows = jnp.stack([-scaled[:, 1], scaled[:, 0]], 1).reshape(row_count, -1)
    matrix = jnp.concatenate([upper_rows, lower_rows], 0)
    stacked = jnp.concatenate([cosine_cols, sine_cols], 1)
    return jnp.dot(stacked, matrix, preferred_element_type=jnp.float32)

def twist_density(panel_density, cosine_y, sine_y):
    density_real = panel_density[:, 0, :, None].astype(jnp.float32)
    density_imag = panel_density[:, 1, :, None].astype(jnp.float32)
    wave_cos = cosine_y.astype(jnp.float32)[:, None, :]
    wave_sin = sine_y.astype(jnp.float32)[:, None, :]
    part_real = wave_cos * density_real + wave_sin * density_imag
    part_imag = wave_cos * density_imag - wave_sin * density_real
    return jnp.stack([part_real, part_imag], 1).reshape(panel_density.shape[0], -1).astype(jnp.bfloat16)

def finish(summed, cosine_y, sine_y, vectors):
    shaped = summed.reshape(summed.shape[0], 2, vectors, -1)
    wave_cos = cosine_y.astype(jnp.float32)[:, None, :]
    wave_sin = sine_y.astype(jnp.float32)[:, None, :]
    far_real = lax.optimization_barrier(jnp.sum(shaped[:, 0] * wave_cos - shaped[:, 1] * wave_sin, -1))
    far_imag = lax.optimization_barrier(jnp.sum(shaped[:, 0] * wave_sin + shaped[:, 1] * wave_cos, -1))
    return jnp.stack([far_real, far_imag], 1)

def combine_near(product, vectors):
    first_half = product[:, 0]
    second = product[:, 1]
    near_real = first_half[:, :vectors] - second[:, vectors:]
    near_imag = second[:, :vectors] + first_half[:, vectors:]
    return jnp.stack([near_real, near_imag], 1)

def panel_sum(values):
    return lax.optimization_barrier(jnp.sum(values, axis=(0, 1, 3)))

def reference(residual, kernel, offsets, neighbor, frequency, lattice_x, lattice_y, spectral_weight):
    column = jnp.arange(GRID_X, dtype=jnp.float32)
    row_index = jnp.arange(GRID_Y, dtype=jnp.float32)
    position_x = ((column[:, None, None] + offsets[:, :, 0, :]) / GRID_X).reshape(-1)
    position_y = ((row_index[None, :, None] + offsets[:, :, 1, :]) / GRID_Y).reshape(-1)
    harmonic_x = (lattice_x - MODES_X // 2).astype(jnp.float32)
    harmonic_y = (lattice_y - MODES_Y // 2).astype(jnp.float32)
    cosine_x, sine_x = phase_table(position_x, harmonic_x)
    cosine_y, sine_y = phase_table(position_y, harmonic_y)
    weight_rows = jnp.take(spectral_weight, frequency[:VECTORS].astype(jnp.int32), axis=0)
    factor = weight_rows * (1.0 / math.sqrt(MODES_X * MODES_Y * PANELS))
    factor_wide = jnp.transpose(factor, (1, 0, 2)).reshape(MODES_X, VECTORS * MODES_Y)[:, None, :]

    def near_field(density):
        candidates = []
        for slot_index in range(9):
            shift_x = slot_index // 3 - 1
            shift_y = slot_index % 3 - 1
            candidates.append(jnp.roll(density, (-shift_x, -shift_y), axis=(0, 1)))
        stacked = jnp.stack(candidates, 2).reshape(GRID_X * GRID_Y, 9, -1)
        picked = jnp.take_along_axis(stacked, neighbor.reshape(GRID_X * GRID_Y, 9, 1), axis=1)
        picked = picked.reshape(GRID_X * GRID_Y, 9, 2 * VECTORS, PANELS_T)
        blocks = kernel.reshape(GRID_X * GRID_Y, 9, 2, PANELS_T, PANELS_T)
        product = jnp.einsum('tjmp,tjcpq->tcmq', picked.astype(jnp.float32), blocks.astype(jnp.float32))
        return combine_near(product, VECTORS).reshape(GRID_X, GRID_Y, 2, VECTORS, PANELS_T)

    def far_field(density):
        panel_density = jnp.transpose(density, (0, 1, 4, 2, 3)).reshape(PANELS, 2, VECTORS)
        twisted = twist_density(panel_density, cosine_y, sine_y)
        coeffs = project_rows(cosine_x, sine_x, twisted)
        scaled = (coeffs * factor_wide).astype(jnp.bfloat16)
        summed = expand_rows(cosine_x, sine_x, scaled)
        far_panel = finish(summed, cosine_y, sine_y, VECTORS)
        return far_panel.reshape(GRID_X, GRID_Y, PANELS_T, 2, VECTORS).transpose(0, 1, 3, 4, 2)

    def apply_operator(density):
        return 0.5 * density.astype(jnp.float32) + near_field(density) + far_field(density)
    squares = panel_sum(residual[:, :, 0] * residual[:, :, 0] + residual[:, :, 1] * residual[:, :, 1])
    basis_scale = jnp.sqrt(squares / PANELS + eps_norm)
    basis_one = (residual / basis_scale[None, None, None, :, None]).astype(jnp.bfloat16)
    image_one = apply_operator(basis_one)
    basis_real = basis_one[:, :, 0].astype(jnp.float32)
    basis_imag = basis_one[:, :, 1].astype(jnp.float32)
    image_real = image_one[:, :, 0]
    image_imag = image_one[:, :, 1]
    coef_real = panel_sum(basis_real * image_real + basis_imag * image_imag) / PANELS
    coef_imag = panel_sum(basis_real * image_imag - basis_imag * image_real) / PANELS
    wide_real = coef_real[None, None, :, None]
    wide_imag = coef_imag[None, None, :, None]
    update_real = image_real - (wide_real * basis_real - wide_imag * basis_imag)
    update_imag = image_imag - (wide_real * basis_imag + wide_imag * basis_real)
    update_sq = panel_sum(update_real * update_real + update_imag * update_imag)
    update_scale = jnp.sqrt(update_sq / PANELS + eps_norm)
    next_basis = (jnp.stack([update_real, update_imag], 2) / update_scale[None, None, None, :, None]).astype(jnp.bfloat16)
    image_two = apply_operator(next_basis)
    arnoldi = jnp.stack([basis_scale, coef_real, coef_imag, update_scale])
    return (image_two, arnoldi)
```

```python
import functools
import math

import jax
import jax.numpy as jnp
from jax import lax
from jax.experimental import pallas as pl
from jax.experimental.pallas import tpu as pltpu
from jax.sharding import PartitionSpec as P

eps_norm = 1e-06
f32 = jnp.float32
bf16 = jnp.bfloat16
MESH = pl.DeviceIdType.MESH

cos_poly = (
    0.9999999890754361,
    -19.739204500992756,
    64.93911749755512,
    -85.45013994334624,
    60.167632824407875,
    -25.967602439336652,
    6.528658637171564,
)
sin_poly = (
    6.283185302518495,
    -41.3417004059728,
    81.60513140266713,
    -76.70301552901445,
    42.02592777896992,
    -14.89984800704947,
    3.2381376825656845,
)


def horner(coefs, z):
    total = coefs[-1] * z + coefs[-2]
    for c in coefs[-3::-1]:
        total = total * z + c
    return total


def cos_sin(turns):
    r = turns - jnp.round(turns)
    z = r * r
    return horner(cos_poly, z), r * horner(sin_poly, z)


def rows_dot(a, b):
    return lax.dot_general(a, b, (((1,), (1,)), ((), ())), preferred_element_type=f32)


def body(
    size_t,
    size_w,
    tiles,
    vectors,
    modes_x,
    modes_y,
    residual,
    blocks,
    offsets,
    neighbor,
    frequency,
    lattice_x,
    lattice_y,
    weight,
    image_out,
    arnoldi_out,
    send_a,
    recv_a,
    send_f1,
    recv_f1,
    send_r,
    recv_r,
    send_b,
    recv_b,
    send_f2,
    recv_f2,
    halo_1,
    halo_2,
    table_x,
    cos_y,
    sin_y,
    harm_x,
    harm_y,
    fact,
    image,
    basis,
    kernel_vmem,
    kernel_sem,
    send_sem,
    recv_sem,
    halo_send,
    halo_recv,
):
    devices = size_t * size_w
    shares = devices // vectors
    rows_b = modes_y // shares
    slots = 2 * tiles
    lanes = 128
    panels = devices * tiles * lanes
    count_x = size_t
    count_y = size_w * tiles
    t = lax.axis_index("tile")
    w = lax.axis_index("wave")
    me = t * size_w + w
    my_vector = me // shares
    my_share = lax.rem(me, shares)

    barrier = pltpu.get_barrier_semaphore()

    def place(index):
        return {"tile": index // size_w, "wave": lax.rem(index, size_w)}

    def greet(k, carry):
        other = lax.rem(me + k, devices)
        pl.semaphore_signal(barrier, inc=1, device_id=place(other), device_id_type=MESH)
        return carry

    lax.fori_loop(1, devices, greet, 0)
    load = pltpu.make_async_copy(blocks, kernel_vmem, kernel_sem)
    load.start()

    def exchange_start(phase, source, target):
        def step(k, carry):
            other = lax.rem(me + k, devices)
            pltpu.make_async_remote_copy(
                src_ref=source(other),
                dst_ref=target.at[me],
                send_sem=send_sem.at[phase],
                recv_sem=recv_sem.at[phase],
                device_id=place(other),
                device_id_type=MESH,
            ).start()
            return carry

        lax.fori_loop(1, devices, step, 0)

    def exchange_wait(phase, target):
        part = target.at[pl.ds(0, devices - 1)]
        pltpu.make_async_copy(part, part, recv_sem.at[phase]).wait()

    def sent_wait(phase, target):
        part = target.at[pl.ds(0, devices - 1)]
        pltpu.make_async_copy(part, part, send_sem.at[phase]).wait()

    up = lax.rem(t + 1, size_t)
    down = lax.rem(t + size_t - 1, size_t)
    other_w = lax.rem(w + 1, size_w)

    def halo_copies(phase, halo):
        copies = []
        targets = ((up, w, 0), (up, other_w, 0), (t, other_w, 1), (down, w, 2), (down, other_w, 2))
        for number, (to_t, to_w, row) in enumerate(targets):
            copies.append(
                pltpu.make_async_remote_copy(
                    src_ref=halo.at[1, pl.ds(w * tiles, tiles)],
                    dst_ref=halo.at[row, pl.ds(w * tiles, tiles)],
                    send_sem=halo_send.at[phase, number],
                    recv_sem=halo_recv.at[phase, number],
                    device_id={"tile": to_t, "wave": to_w},
                    device_id_type=MESH,
                )
            )
        return copies

    def stage(values, halo, slab):
        for h in range(tiles):
            rounded = [values[h][c].astype(bf16) for c in range(2)]
            for c in range(2):
                wide = rounded[c].astype(f32)
                basis[h, c] = wide
                slab[:, c * tiles + h, :] = wide
            halo[1, w * tiles + h] = jnp.concatenate(rounded, 0)

    first = [[residual[h, c] for c in range(2)] for h in range(tiles)]
    stage(first, halo_1, send_a)
    offset_rows = offsets[...].reshape(slots, lanes)
    for v in range(vectors):
        send_a[v, slots : 2 * slots, :] = offset_rows
    pl.semaphore_wait(barrier, devices - 1)
    copies_1 = halo_copies(0, halo_1)
    exchange_start(0, lambda other: send_a.at[other // shares], recv_a)
    for copy in copies_1:
        copy.start()
    recv_a[me] = send_a[my_vector]

    square = jnp.zeros((vectors, lanes), f32)
    for h in range(tiles):
        for c in range(2):
            square += residual[h, c] * residual[h, c]

    wave_x = (lattice_x[...] - modes_x // 2).astype(f32)
    harm_x[...] = jnp.broadcast_to(wave_x, (lanes, modes_x)).T
    wave_y = (lattice_y[...] - modes_y // 2).astype(f32)
    harm_y[...] = jnp.broadcast_to(wave_y, (lanes, modes_y)).T
    my_weight = weight[frequency[my_vector]]
    fact[...] = (my_weight * (1.0 / math.sqrt(modes_x * modes_y * panels))).T
    share_rows = pl.ds(pl.multiple_of(my_share * rows_b, rows_b), rows_b)
    hx = harm_x[...]
    hy = harm_y[share_rows, :]
    factor = fact[share_rows, :]

    exchange_wait(0, recv_a)

    def project(with_tables, recv):
        def step(d, total):
            twisted = []
            for h in range(tiles):
                cols = slice(h * lanes, (h + 1) * lanes)
                if with_tables:
                    g = (d // size_w).astype(f32)
                    column = (lax.rem(d, size_w) * tiles + h).astype(f32)
                    off_x = recv[d, slots + 2 * h : slots + 2 * h + 1, :]
                    off_y = recv[d, slots + 2 * h + 1 : slots + 2 * h + 2, :]
                    px = (g + off_x) / count_x
                    py = (column + off_y) / count_y
                    cos_a, sin_a = cos_sin(px * hx)
                    table_x[d, 0:modes_x, cols] = cos_a.astype(bf16)
                    table_x[d, modes_x : 2 * modes_x, cols] = sin_a.astype(bf16)
                    cos_b, sin_b = cos_sin(py * hy)
                    cy = cos_b.astype(bf16).astype(f32)
                    sy = sin_b.astype(bf16).astype(f32)
                    cos_y[d, :, cols] = cy
                    sin_y[d, :, cols] = sy
                else:
                    cy = cos_y[d, :, cols]
                    sy = sin_y[d, :, cols]
                q_r = recv[d, h : h + 1, :]
                q_i = recv[d, tiles + h : tiles + h + 1, :]
                twisted.append(
                    jnp.concatenate([cy * q_r + sy * q_i, cy * q_i - sy * q_r], 0).astype(bf16)
                )
            return total + rows_dot(jnp.concatenate(twisted, 1), table_x[d])

        return lax.fori_loop(0, devices, step, jnp.zeros((2 * rows_b, 2 * modes_x), f32))

    def far_partial(total, slab):
        top = total[:rows_b]
        low = total[rows_b:]
        real = top[:, :modes_x] + low[:, modes_x:]
        imag = low[:, :modes_x] - top[:, modes_x:]
        real = (real * factor).astype(bf16)
        imag = (imag * factor).astype(bf16)
        matrix = jnp.concatenate(
            [jnp.concatenate([real, -imag], 1), jnp.concatenate([imag, real], 1)], 0
        )

        def step(d, carry):
            summed = jnp.dot(matrix, table_x[d], preferred_element_type=f32)
            s_r = summed[:rows_b]
            s_i = summed[rows_b:]
            cy = cos_y[d]
            sy = sin_y[d]
            far_r = jnp.sum(s_r * cy - s_i * sy, 0, keepdims=True)
            far_i = jnp.sum(s_r * sy + s_i * cy, 0, keepdims=True)
            for h in range(tiles):
                cols = slice(h * lanes, (h + 1) * lanes)
                slab[d, h : h + 1, :] = far_r[:, cols]
                slab[d, tiles + h : tiles + h + 1, :] = far_i[:, cols]
            return carry

        lax.fori_loop(0, devices, step, 0)

    def near_and_half(halo):
        for h in range(tiles):
            picked = []
            for j in range(9):
                slot = neighbor[h * 9 + j]
                row = slot // 3
                column = lax.rem(w * tiles + h + lax.rem(slot, 3) - 1 + count_y, count_y)
                picked.append(halo[row, column])
            left = jnp.concatenate(picked, 1)
            right = jnp.concatenate(
                [
                    jnp.concatenate([kernel_vmem[h, j, c] for j in range(9)], 0)
                    for c in range(2)
                ],
                1,
            )
            product = jnp.dot(left, right, preferred_element_type=f32)
            image[h, 0] = (
                0.5 * basis[h, 0] + product[:vectors, :lanes] - product[vectors:, lanes:]
            )
            image[h, 1] = (
                0.5 * basis[h, 1] + product[:vectors, lanes:] + product[vectors:, :lanes]
            )

    def far_of(recv, row):
        grouped = recv[:, row, :].reshape(vectors, shares, lanes)
        return jnp.sum(grouped, 1)

    def far_own(slab, recv):
        recv[me, 0:slots, :] = slab[me, 0:slots, :]

    far_partial(project(True, recv_a), send_f1)
    exchange_start(1, lambda other: send_f1.at[other], recv_f1)
    far_own(send_f1, recv_f1)
    load.wait()
    for copy in copies_1:
        copy.wait_recv()
    near_and_half(halo_1)
    exchange_wait(1, recv_f1)

    inner_r = jnp.zeros((vectors, lanes), f32)
    inner_i = jnp.zeros((vectors, lanes), f32)
    for h in range(tiles):
        w_r = image[h, 0] + far_of(recv_f1, h)
        w_i = image[h, 1] + far_of(recv_f1, tiles + h)
        image[h, 0] = w_r
        image[h, 1] = w_i
        b_r = basis[h, 0]
        b_i = basis[h, 1]
        inner_r += b_r * w_r + b_i * w_i
        inner_i += b_r * w_i - b_i * w_r
    lane = lax.broadcasted_iota(jnp.int32, (vectors, lanes), 1)
    sums = [jnp.sum(x, 1, keepdims=True) for x in (square, inner_r, inner_i)]
    send_r[...] = jnp.where(lane == 0, sums[0], jnp.where(lane == 1, sums[1], sums[2]))
    exchange_start(2, lambda other: send_r, recv_r)
    recv_r[me] = send_r[...]
    exchange_wait(2, recv_r)
    sums = jnp.sum(recv_r[...], 0)
    scale = jnp.sqrt(sums[:, 0:1] / panels + eps_norm)
    inverse = 1.0 / scale
    inverse_2 = inverse * inverse
    coef_r = sums[:, 1:2] / panels * inverse_2
    coef_i = sums[:, 2:3] / panels * inverse_2

    square = jnp.zeros((vectors, lanes), f32)
    second = []
    for h in range(tiles):
        b_r = basis[h, 0]
        b_i = basis[h, 1]
        u_r = (image[h, 0] - (coef_r * b_r - coef_i * b_i)) * inverse
        u_i = (image[h, 1] - (coef_r * b_i + coef_i * b_r)) * inverse
        square += u_r * u_r + u_i * u_i
        second.append((u_r, u_i))
    stage(second, halo_2, send_b)
    copies_2 = halo_copies(1, halo_2)
    exchange_start(3, lambda other: send_b.at[other // shares], recv_b)
    for copy in copies_2:
        copy.start()
    recv_b[me] = send_b[my_vector]

    def put_square(d, carry):
        send_f2[d, slots : slots + vectors, :] = square
        return carry

    lax.fori_loop(0, devices, put_square, 0)
    exchange_wait(3, recv_b)
    far_partial(project(False, recv_b), send_f2)
    exchange_start(4, lambda other: send_f2.at[other], recv_f2)
    recv_f2[me] = send_f2[me]
    for copy in copies_2:
        copy.wait_recv()
    near_and_half(halo_2)
    exchange_wait(4, recv_f2)
    update_sq = jnp.sum(recv_f2[:, slots : slots + vectors, :], 0)
    update_sq = jnp.sum(update_sq, 1, keepdims=True)
    update_scale = jnp.sqrt(update_sq / panels + eps_norm)
    inverse = 1.0 / update_scale
    for h in range(tiles):
        for c in range(2):
            image_out[h, c] = (image[h, c] + far_of(recv_f2, c * tiles + h)) * inverse
    row = lax.broadcasted_iota(jnp.int32, (vectors, lanes), 0)
    for number, value in enumerate((scale, coef_r, coef_i, update_scale)):
        line = jnp.sum(jnp.where(row == lane, value, 0.0), 0, keepdims=True)
        arnoldi_out[number : number + 1, :] = line[:, :vectors]

    for copy in copies_1 + copies_2:
        copy.wait_send()
    for phase, target in enumerate((recv_a, recv_f1, recv_r, recv_b, recv_f2)):
        sent_wait(phase, target)


def per_device(
    size_t,
    size_w,
    residual,
    kernel,
    offsets,
    neighbor,
    frequency,
    lattice_x,
    lattice_y,
    spectral_weight,
):
    strips, tiles, _, vectors, lanes = residual.shape
    modes_x, modes_y = spectral_weight.shape[1:]
    devices = size_t * size_w
    assert strips == 1 and lanes == 128 and size_w == 2 and size_t > 2
    assert devices % vectors == 0
    rows_b = modes_y // (devices // vectors)
    slots = 2 * tiles
    vmem = pl.BlockSpec(memory_space=pltpu.VMEM)
    smem = pl.BlockSpec(memory_space=pltpu.SMEM)
    halo = pltpu.VMEM((3, size_w * tiles, 2 * vectors, lanes), bf16)
    image, arnoldi = pl.pallas_call(
        functools.partial(body, size_t, size_w, tiles, vectors, modes_x, modes_y),
        out_shape=(
            jax.ShapeDtypeStruct((tiles, 2, vectors, lanes), f32),
            jax.ShapeDtypeStruct((4, vectors), f32),
        ),
        in_specs=[
            vmem,
            pl.BlockSpec(memory_space=pl.ANY),
            vmem,
            smem,
            smem,
            vmem,
            vmem,
            vmem,
        ],
        out_specs=(vmem, vmem),
        scratch_shapes=[
            pltpu.VMEM((vectors, 2 * slots, lanes), f32),
            pltpu.VMEM((devices, 2 * slots, lanes), f32),
            pltpu.VMEM((devices, slots, lanes), f32),
            pltpu.VMEM((devices, slots, lanes), f32),
            pltpu.VMEM((vectors, lanes), f32),
            pltpu.VMEM((devices, vectors, lanes), f32),
            pltpu.VMEM((vectors, slots, lanes), f32),
            pltpu.VMEM((devices, slots, lanes), f32),
            pltpu.VMEM((devices, slots + vectors, lanes), f32),
            pltpu.VMEM((devices, slots + vectors, lanes), f32),
            halo,
            halo,
            pltpu.VMEM((devices, 2 * modes_x, tiles * lanes), bf16),
            pltpu.VMEM((devices, rows_b, tiles * lanes), f32),
            pltpu.VMEM((devices, rows_b, tiles * lanes), f32),
            pltpu.VMEM((modes_x, lanes), f32),
            pltpu.VMEM((modes_y, lanes), f32),
            pltpu.VMEM((modes_y, modes_x), f32),
            pltpu.VMEM((tiles, 2, vectors, lanes), f32),
            pltpu.VMEM((tiles, 2, vectors, lanes), f32),
            pltpu.VMEM((tiles, 9, 2, lanes, lanes), bf16),
            pltpu.SemaphoreType.DMA,
            pltpu.SemaphoreType.DMA((5,)),
            pltpu.SemaphoreType.DMA((5,)),
            pltpu.SemaphoreType.DMA((2, 5)),
            pltpu.SemaphoreType.DMA((2, 5)),
        ],
        compiler_params=pltpu.CompilerParams(
            collective_id=0, has_side_effects=True, vmem_limit_bytes=56 * 1024 * 1024
        ),
        name="arnoldi_pair",
    )(
        residual[0],
        kernel[0],
        offsets[0],
        neighbor.reshape(-1),
        frequency,
        lattice_x[None],
        lattice_y[None],
        spectral_weight,
    )
    return image[None], arnoldi


def solution(mesh):
    return jax.shard_map(
        functools.partial(per_device, mesh.shape["tile"], mesh.shape["wave"]),
        mesh=mesh,
        in_specs=(
            P(("grp", "tile"), "wave", None, None, None),
            P(("grp", "tile"), "wave", None, None, None, None),
            P(("grp", "tile"), "wave", None, None),
            P(("grp", "tile"), "wave", None),
            P("grp"),
            P(),
            P(),
            P(),
        ),
        out_specs=(P(("grp", "tile"), "wave", None, None, None), P("grp", None)),
        check_vma=False,
    )
```

```python
import functools
import math

import jax
import jax.numpy as jnp
from jax import lax
from jax.experimental import pallas as pl
from jax.experimental.pallas import tpu as pltpu
from jax.sharding import PartitionSpec as P

eps_norm = 1e-06
unroll_project = 8
unroll_expand = 5
f32 = jnp.float32
bf16 = jnp.bfloat16
MESH = pl.DeviceIdType.MESH

cos_poly = (
    0.9999999890754361,
    -19.739204500992756,
    64.93911749755512,
    -85.45013994334624,
    60.167632824407875,
    -25.967602439336652,
    6.528658637171564,
)
sin_poly = (
    6.283185302518495,
    -41.3417004059728,
    81.60513140266713,
    -76.70301552901445,
    42.02592777896992,
    -14.89984800704947,
    3.2381376825656845,
)


def horner(coefs, z):
    total = coefs[-1] * z + coefs[-2]
    for c in coefs[-3::-1]:
        total = total * z + c
    return total


def cos_sin(turns):
    r = turns - jnp.round(turns)
    z = r * r
    return horner(cos_poly, z), r * horner(sin_poly, z)


def rows_dot(a, b):
    return lax.dot_general(a, b, (((1,), (1,)), ((), ())), preferred_element_type=f32)


def body(
    size_t,
    size_w,
    tiles,
    vectors,
    modes_x,
    modes_y,
    residual,
    blocks,
    offsets,
    neighbor,
    frequency,
    lattice_x,
    lattice_y,
    weight,
    image_out,
    arnoldi_out,
    send_a,
    recv_a,
    send_f1,
    recv_f1,
    send_r,
    recv_r,
    send_b,
    recv_b,
    send_f2,
    recv_f2,
    halo_1,
    halo_2,
    table_x,
    cos_y,
    sin_y,
    harm_x,
    harm_y,
    fact,
    image,
    basis,
    kernel_vmem,
    kernel_sem,
    send_sem,
    recv_sem,
    halo_send,
    halo_recv,
):
    devices = size_t * size_w
    shares = devices // vectors
    rows_b = modes_y // shares
    slots = 2 * tiles
    lanes = 128
    panels = devices * tiles * lanes
    count_x = size_t
    count_y = size_w * tiles
    t = lax.axis_index("tile")
    w = lax.axis_index("wave")
    me = t * size_w + w
    my_vector = me // shares
    my_share = lax.rem(me, shares)

    barrier = pltpu.get_barrier_semaphore()

    def place(index):
        return {"tile": index // size_w, "wave": lax.rem(index, size_w)}

    def greet(k, carry):
        other = lax.rem(me + k, devices)
        pl.semaphore_signal(barrier, inc=1, device_id=place(other), device_id_type=MESH)
        return carry

    lax.fori_loop(1, devices, greet, 0)
    load = pltpu.make_async_copy(blocks, kernel_vmem, kernel_sem)
    load.start()

    def copy_to(phase, other, source, target):
        return pltpu.make_async_remote_copy(
            src_ref=source,
            dst_ref=target.at[me],
            send_sem=send_sem.at[phase],
            recv_sem=recv_sem.at[phase],
            device_id=place(other),
            device_id_type=MESH,
        )

    def exchange_start(phase, source, target):
        def step(k, carry):
            other = lax.rem(me + k, devices)
            copy_to(phase, other, source(other), target).start()
            return carry

        lax.fori_loop(1, devices, step, 0)

    def exchange_wait(phase, target):
        part = target.at[pl.ds(0, devices - 1)]
        pltpu.make_async_copy(part, part, recv_sem.at[phase]).wait()

    def sent_wait(phase, target):
        part = target.at[pl.ds(0, devices - 1)]
        pltpu.make_async_copy(part, part, send_sem.at[phase]).wait()

    up = lax.rem(t + 1, size_t)
    down = lax.rem(t + size_t - 1, size_t)
    other_w = lax.rem(w + 1, size_w)

    def halo_copies(phase, halo):
        copies = []
        targets = ((up, w, 0), (up, other_w, 0), (t, other_w, 1), (down, w, 2), (down, other_w, 2))
        for number, (to_t, to_w, row) in enumerate(targets):
            copies.append(
                pltpu.make_async_remote_copy(
                    src_ref=halo.at[1, pl.ds(w * tiles, tiles)],
                    dst_ref=halo.at[row, pl.ds(w * tiles, tiles)],
                    send_sem=halo_send.at[phase, number],
                    recv_sem=halo_recv.at[phase, number],
                    device_id={"tile": to_t, "wave": to_w},
                    device_id_type=MESH,
                )
            )
        return copies

    def stage(values, halo, slab):
        for h in range(tiles):
            rounded = [values[h][c].astype(bf16) for c in range(2)]
            for c in range(2):
                wide = rounded[c].astype(f32)
                basis[h, c] = wide
                slab[:, c * tiles + h, :] = wide
            halo[1, w * tiles + h] = jnp.concatenate(rounded, 0)

    first = [[residual[h, c] for c in range(2)] for h in range(tiles)]
    stage(first, halo_1, send_a)
    offset_rows = offsets[...].reshape(slots, lanes)
    for v in range(vectors):
        send_a[v, slots : 2 * slots, :] = offset_rows
    pl.semaphore_wait(barrier, devices - 1)
    copies_1 = halo_copies(0, halo_1)
    exchange_start(0, lambda other: send_a.at[other // shares], recv_a)
    for copy in copies_1:
        copy.start()
    recv_a[me] = send_a[my_vector]

    square = jnp.zeros((vectors, lanes), f32)
    for h in range(tiles):
        for c in range(2):
            square += residual[h, c] * residual[h, c]

    wave_x = (lattice_x[...] - modes_x // 2).astype(f32)
    harm_x[...] = jnp.broadcast_to(wave_x, (lanes, modes_x)).T
    wave_y = (lattice_y[...] - modes_y // 2).astype(f32)
    harm_y[...] = jnp.broadcast_to(wave_y, (lanes, modes_y)).T
    my_weight = weight[frequency[my_vector]]
    fact[...] = (my_weight * (1.0 / math.sqrt(modes_x * modes_y * panels))).T
    share_rows = pl.ds(pl.multiple_of(my_share * rows_b, rows_b), rows_b)
    hx = harm_x[...]
    hy = harm_y[share_rows, :]
    factor = fact[share_rows, :]

    exchange_wait(0, recv_a)

    def project(with_tables, recv):
        def step(d, total):
            twisted = []
            for h in range(tiles):
                cols = slice(h * lanes, (h + 1) * lanes)
                if with_tables:
                    g = (d // size_w).astype(f32)
                    column = (lax.rem(d, size_w) * tiles + h).astype(f32)
                    off_x = recv[d, slots + 2 * h : slots + 2 * h + 1, :]
                    off_y = recv[d, slots + 2 * h + 1 : slots + 2 * h + 2, :]
                    px = (g + off_x) / count_x
                    py = (column + off_y) / count_y
                    cos_a, sin_a = cos_sin(px * hx)
                    table_x[d, 0:modes_x, cols] = cos_a.astype(bf16)
                    table_x[d, modes_x : 2 * modes_x, cols] = sin_a.astype(bf16)
                    cos_b, sin_b = cos_sin(py * hy)
                    cy = cos_b.astype(bf16).astype(f32)
                    sy = sin_b.astype(bf16).astype(f32)
                    cos_y[d, :, cols] = cy
                    sin_y[d, :, cols] = sy
                else:
                    cy = cos_y[d, :, cols]
                    sy = sin_y[d, :, cols]
                q_r = recv[d, h : h + 1, :]
                q_i = recv[d, tiles + h : tiles + h + 1, :]
                twisted.append(
                    jnp.concatenate([cy * q_r + sy * q_i, cy * q_i - sy * q_r], 0).astype(bf16)
                )
            return total + rows_dot(jnp.concatenate(twisted, 1), table_x[d])

        zero = jnp.zeros((2 * rows_b, 2 * modes_x), f32)
        return lax.fori_loop(0, devices, step, zero, unroll=unroll_project)

    def far_partial(total, slab, phase, target):
        top = total[:rows_b]
        low = total[rows_b:]
        real = top[:, :modes_x] + low[:, modes_x:]
        imag = low[:, :modes_x] - top[:, modes_x:]
        real = (real * factor).astype(bf16)
        imag = (imag * factor).astype(bf16)
        matrix = jnp.concatenate(
            [jnp.concatenate([real, -imag], 1), jnp.concatenate([imag, real], 1)], 0
        )

        def expand(d):
            summed = jnp.dot(matrix, table_x[d], preferred_element_type=f32)
            s_r = summed[:rows_b]
            s_i = summed[rows_b:]
            cy = cos_y[d]
            sy = sin_y[d]
            far_r = jnp.sum(s_r * cy - s_i * sy, 0, keepdims=True)
            far_i = jnp.sum(s_r * sy + s_i * cy, 0, keepdims=True)
            for h in range(tiles):
                cols = slice(h * lanes, (h + 1) * lanes)
                slab[d, h : h + 1, :] = far_r[:, cols]
                slab[d, tiles + h : tiles + h + 1, :] = far_i[:, cols]

        def step(k, carry):
            d = lax.rem(me + k, devices)
            expand(d)
            copy_to(phase, d, slab.at[d], target).start()
            return carry

        lax.fori_loop(1, devices, step, 0, unroll=unroll_expand)
        expand(me)

    def near_and_half(halo):
        for h in range(tiles):
            picked = []
            for j in range(9):
                slot = neighbor[0, h, j]
                row = slot // 3
                column = lax.rem(w * tiles + h + lax.rem(slot, 3) - 1 + count_y, count_y)
                picked.append(halo[row, column])
            left = jnp.concatenate(picked, 1)
            right = jnp.concatenate(
                [
                    jnp.concatenate([kernel_vmem[h, j, c] for j in range(9)], 0)
                    for c in range(2)
                ],
                1,
            )
            product = jnp.dot(left, right, preferred_element_type=f32)
            image[h, 0] = (
                0.5 * basis[h, 0] + product[:vectors, :lanes] - product[vectors:, lanes:]
            )
            image[h, 1] = (
                0.5 * basis[h, 1] + product[:vectors, lanes:] + product[vectors:, :lanes]
            )

    def far_of(recv, row):
        grouped = recv[:, row, :].reshape(vectors, shares, lanes)
        return jnp.sum(grouped, 1)

    def far_own(slab, recv):
        recv[me, 0:slots, :] = slab[me, 0:slots, :]

    far_partial(project(True, recv_a), send_f1, 1, recv_f1)
    far_own(send_f1, recv_f1)
    load.wait()
    for copy in copies_1:
        copy.wait_recv()
    near_and_half(halo_1)
    exchange_wait(1, recv_f1)

    inner_r = jnp.zeros((vectors, lanes), f32)
    inner_i = jnp.zeros((vectors, lanes), f32)
    for h in range(tiles):
        w_r = image[h, 0] + far_of(recv_f1, h)
        w_i = image[h, 1] + far_of(recv_f1, tiles + h)
        image[h, 0] = w_r
        image[h, 1] = w_i
        b_r = basis[h, 0]
        b_i = basis[h, 1]
        inner_r += b_r * w_r + b_i * w_i
        inner_i += b_r * w_i - b_i * w_r
    lane = lax.broadcasted_iota(jnp.int32, (vectors, lanes), 1)
    sums = [jnp.sum(x, 1, keepdims=True) for x in (square, inner_r, inner_i)]
    send_r[...] = jnp.where(lane == 0, sums[0], jnp.where(lane == 1, sums[1], sums[2]))
    exchange_start(2, lambda other: send_r, recv_r)
    recv_r[me] = send_r[...]
    exchange_wait(2, recv_r)
    sums = jnp.sum(recv_r[...], 0)
    scale = jnp.sqrt(sums[:, 0:1] / panels + eps_norm)
    inverse = 1.0 / scale
    inverse_2 = inverse * inverse
    coef_r = sums[:, 1:2] / panels * inverse_2
    coef_i = sums[:, 2:3] / panels * inverse_2

    square = jnp.zeros((vectors, lanes), f32)
    second = []
    for h in range(tiles):
        b_r = basis[h, 0]
        b_i = basis[h, 1]
        u_r = (image[h, 0] - (coef_r * b_r - coef_i * b_i)) * inverse
        u_i = (image[h, 1] - (coef_r * b_i + coef_i * b_r)) * inverse
        square += u_r * u_r + u_i * u_i
        second.append((u_r, u_i))
    stage(second, halo_2, send_b)
    copies_2 = halo_copies(1, halo_2)
    exchange_start(3, lambda other: send_b.at[other // shares], recv_b)
    for copy in copies_2:
        copy.start()
    recv_b[me] = send_b[my_vector]

    def put_square(d, carry):
        send_f2[d, slots : slots + vectors, :] = square
        return carry

    lax.fori_loop(0, devices, put_square, 0)
    exchange_wait(3, recv_b)
    far_partial(project(False, recv_b), send_f2, 4, recv_f2)
    recv_f2[me] = send_f2[me]
    for copy in copies_2:
        copy.wait_recv()
    near_and_half(halo_2)
    exchange_wait(4, recv_f2)
    update_sq = jnp.sum(recv_f2[:, slots : slots + vectors, :], 0)
    update_sq = jnp.sum(update_sq, 1, keepdims=True)
    update_scale = jnp.sqrt(update_sq / panels + eps_norm)
    inverse = 1.0 / update_scale
    for h in range(tiles):
        for c in range(2):
            image_out[h, c] = (image[h, c] + far_of(recv_f2, c * tiles + h)) * inverse
    row = lax.broadcasted_iota(jnp.int32, (vectors, lanes), 0)
    for number, value in enumerate((scale, coef_r, coef_i, update_scale)):
        line = jnp.sum(jnp.where(row == lane, value, 0.0), 0, keepdims=True)
        arnoldi_out[number : number + 1, :] = line[:, :vectors]

    for copy in copies_1 + copies_2:
        copy.wait_send()
    for phase, target in enumerate((recv_a, recv_f1, recv_r, recv_b, recv_f2)):
        sent_wait(phase, target)


def hand_over(image, arnoldi, image_out, arnoldi_out):
    image_out[...] = image[...]
    arnoldi_out[...] = arnoldi[...]


def per_device(
    size_t,
    size_w,
    residual,
    kernel,
    offsets,
    neighbor,
    frequency,
    lattice_x,
    lattice_y,
    spectral_weight,
):
    strips, tiles, _, vectors, lanes = residual.shape
    modes_x, modes_y = spectral_weight.shape[1:]
    devices = size_t * size_w
    assert strips == 1 and lanes == 128 and size_w == 2 and size_t > 2
    assert devices % vectors == 0
    rows_b = modes_y // (devices // vectors)
    slots = 2 * tiles
    vmem = pl.BlockSpec(memory_space=pltpu.VMEM)
    smem = pl.BlockSpec(memory_space=pltpu.SMEM)
    halo = pltpu.VMEM((3, size_w * tiles, 2 * vectors, lanes), bf16)
    image, arnoldi = pl.pallas_call(
        functools.partial(body, size_t, size_w, tiles, vectors, modes_x, modes_y),
        out_shape=(
            jax.ShapeDtypeStruct((tiles, 2, vectors, lanes), f32),
            jax.ShapeDtypeStruct((4, vectors), f32),
        ),
        in_specs=[
            vmem,
            pl.BlockSpec(memory_space=pl.ANY),
            vmem,
            smem,
            smem,
            vmem,
            vmem,
            vmem,
        ],
        out_specs=(vmem, vmem),
        scratch_shapes=[
            pltpu.VMEM((vectors, 2 * slots, lanes), f32),
            pltpu.VMEM((devices, 2 * slots, lanes), f32),
            pltpu.VMEM((devices, slots, lanes), f32),
            pltpu.VMEM((devices, slots, lanes), f32),
            pltpu.VMEM((vectors, lanes), f32),
            pltpu.VMEM((devices, vectors, lanes), f32),
            pltpu.VMEM((vectors, slots, lanes), f32),
            pltpu.VMEM((devices, slots, lanes), f32),
            pltpu.VMEM((devices, slots + vectors, lanes), f32),
            pltpu.VMEM((devices, slots + vectors, lanes), f32),
            halo,
            halo,
            pltpu.VMEM((devices, 2 * modes_x, tiles * lanes), bf16),
            pltpu.VMEM((devices, rows_b, tiles * lanes), f32),
            pltpu.VMEM((devices, rows_b, tiles * lanes), f32),
            pltpu.VMEM((modes_x, lanes), f32),
            pltpu.VMEM((modes_y, lanes), f32),
            pltpu.VMEM((modes_y, modes_x), f32),
            pltpu.VMEM((tiles, 2, vectors, lanes), f32),
            pltpu.VMEM((tiles, 2, vectors, lanes), f32),
            pltpu.VMEM((tiles, 9, 2, lanes, lanes), bf16),
            pltpu.SemaphoreType.DMA,
            pltpu.SemaphoreType.DMA((5,)),
            pltpu.SemaphoreType.DMA((5,)),
            pltpu.SemaphoreType.DMA((2, 5)),
            pltpu.SemaphoreType.DMA((2, 5)),
        ],
        compiler_params=pltpu.CompilerParams(
            collective_id=0, has_side_effects=True, vmem_limit_bytes=56 * 1024 * 1024
        ),
        name="arnoldi_pair",
    )(
        residual[0],
        kernel[0],
        offsets[0],
        neighbor,
        frequency,
        lattice_x[None],
        lattice_y[None],
        spectral_weight,
    )
    image, arnoldi = pl.pallas_call(
        hand_over,
        out_shape=(
            jax.ShapeDtypeStruct(image.shape, f32),
            jax.ShapeDtypeStruct(arnoldi.shape, f32),
        ),
        in_specs=[vmem, vmem],
        out_specs=(vmem, vmem),
        name="hand_over",
    )(image, arnoldi)
    return image[None], arnoldi


def solution(mesh):
    return jax.shard_map(
        functools.partial(per_device, mesh.shape["tile"], mesh.shape["wave"]),
        mesh=mesh,
        in_specs=(
            P(("grp", "tile"), "wave", None, None, None),
            P(("grp", "tile"), "wave", None, None, None, None),
            P(("grp", "tile"), "wave", None, None),
            P(("grp", "tile"), "wave", None),
            P("grp"),
            P(),
            P(),
            P(),
        ),
        out_specs=(P(("grp", "tile"), "wave", None, None, None), P("grp", None)),
        check_vma=False,
    )
```

```python
import functools
import math

import jax
import jax.numpy as jnp
from jax import lax
from jax.experimental import pallas as pl
from jax.experimental.pallas import tpu as pltpu
from jax.sharding import PartitionSpec as P

eps_norm = 1e-06
unroll_project = 8
unroll_expand = 5
f32 = jnp.float32
bf16 = jnp.bfloat16
MESH = pl.DeviceIdType.MESH

cos_poly = (
    0.9999999890754361,
    -19.739204500992756,
    64.93911749755512,
    -85.45013994334624,
    60.167632824407875,
    -25.967602439336652,
    6.528658637171564,
)
sin_poly = (
    6.283185302518495,
    -41.3417004059728,
    81.60513140266713,
    -76.70301552901445,
    42.02592777896992,
    -14.89984800704947,
    3.2381376825656845,
)


def horner(coefs, z):
    total = coefs[-1] * z + coefs[-2]
    for c in coefs[-3::-1]:
        total = total * z + c
    return total


def cos_sin(turns):
    r = turns - jnp.round(turns)
    z = r * r
    return horner(cos_poly, z), r * horner(sin_poly, z)


def rows_dot(a, b):
    return lax.dot_general(a, b, (((1,), (1,)), ((), ())), preferred_element_type=f32)


def body(
    size_t,
    size_w,
    tiles,
    vectors,
    modes_x,
    modes_y,
    residual,
    blocks,
    offsets,
    neighbor,
    frequency,
    lattice_x,
    lattice_y,
    weight,
    image_out,
    arnoldi_out,
    send_a,
    recv_a,
    send_f1,
    recv_f1,
    send_r,
    recv_r,
    send_b,
    recv_b,
    send_f2,
    recv_f2,
    halo_1,
    halo_2,
    table_x,
    cos_y,
    sin_y,
    fact,
    image,
    basis,
    kernel_vmem,
    kernel_sem,
    send_sem,
    recv_sem,
    halo_send,
    halo_recv,
):
    devices = size_t * size_w
    shares = devices // vectors
    rows_b = modes_y // shares
    slots = 2 * tiles
    lanes = 128
    panels = devices * tiles * lanes
    count_x = size_t
    count_y = size_w * tiles
    t = lax.axis_index("tile")
    w = lax.axis_index("wave")
    me = t * size_w + w
    my_vector = me // shares
    my_share = lax.rem(me, shares)

    barrier = pltpu.get_barrier_semaphore()

    def place(index):
        return {"tile": index // size_w, "wave": lax.rem(index, size_w)}

    def greet(k, carry):
        other = lax.rem(me + k, devices)
        pl.semaphore_signal(barrier, inc=1, device_id=place(other), device_id_type=MESH)
        return carry

    lax.fori_loop(1, devices, greet, 0)
    load = pltpu.make_async_copy(blocks, kernel_vmem, kernel_sem)
    load.start()

    def copy_to(phase, other, source, target):
        return pltpu.make_async_remote_copy(
            src_ref=source,
            dst_ref=target.at[me],
            send_sem=send_sem.at[phase],
            recv_sem=recv_sem.at[phase],
            device_id=place(other),
            device_id_type=MESH,
        )

    def exchange_start(phase, source, target):
        def step(k, carry):
            other = lax.rem(me + k, devices)
            copy_to(phase, other, source(other), target).start()
            return carry

        lax.fori_loop(1, devices, step, 0)

    def exchange_wait(phase, target):
        part = target.at[pl.ds(0, devices - 1)]
        pltpu.make_async_copy(part, part, recv_sem.at[phase]).wait()

    def sent_wait(phase, target):
        part = target.at[pl.ds(0, devices - 1)]
        pltpu.make_async_copy(part, part, send_sem.at[phase]).wait()

    up = lax.rem(t + 1, size_t)
    down = lax.rem(t + size_t - 1, size_t)
    other_w = lax.rem(w + 1, size_w)

    def halo_copies(phase, halo):
        copies = []
        targets = ((up, w, 0), (up, other_w, 0), (t, other_w, 1), (down, w, 2), (down, other_w, 2))
        for number, (to_t, to_w, row) in enumerate(targets):
            copies.append(
                pltpu.make_async_remote_copy(
                    src_ref=halo.at[1, pl.ds(w * tiles, tiles)],
                    dst_ref=halo.at[row, pl.ds(w * tiles, tiles)],
                    send_sem=halo_send.at[phase, number],
                    recv_sem=halo_recv.at[phase, number],
                    device_id={"tile": to_t, "wave": to_w},
                    device_id_type=MESH,
                )
            )
        return copies

    def stage(values, halo, slab):
        for h in range(tiles):
            rounded = [values[h][c].astype(bf16) for c in range(2)]
            for c in range(2):
                wide = rounded[c].astype(f32)
                basis[h, c] = wide
                slab[:, c * tiles + h, :] = wide
            halo[1, w * tiles + h] = jnp.concatenate(rounded, 0)

    first = [[residual[h, c] for c in range(2)] for h in range(tiles)]
    stage(first, halo_1, send_a)
    offset_rows = offsets[...].reshape(slots, lanes)
    for v in range(vectors):
        send_a[v, slots : 2 * slots, :] = offset_rows
    pl.semaphore_wait(barrier, devices - 1)
    copies_1 = halo_copies(0, halo_1)
    exchange_start(0, lambda other: send_a.at[other // shares], recv_a)
    for copy in copies_1:
        copy.start()
    recv_a[me] = send_a[my_vector]

    square = jnp.zeros((vectors, lanes), f32)
    for h in range(tiles):
        for c in range(2):
            square += residual[h, c] * residual[h, c]

    my_weight = weight[frequency[my_vector]] * (1.0 / math.sqrt(modes_x * modes_y * panels))
    row_y = lax.broadcasted_iota(jnp.int32, (modes_y, modes_y), 0)
    row_x = lax.broadcasted_iota(jnp.int32, (modes_x, modes_x), 0)
    pick_y = jnp.where(jnp.broadcast_to(lattice_y[...], row_y.shape) == row_y, 1.0, 0.0)
    pick_x = jnp.where(jnp.broadcast_to(lattice_x[...], row_x.shape) == row_x, 1.0, 0.0)
    exact = lax.Precision.HIGHEST
    by_y = jnp.dot(pick_y, my_weight.T, precision=exact, preferred_element_type=f32)
    fact[...] = jnp.dot(by_y, pick_x.T, precision=exact, preferred_element_type=f32)
    first_y = my_share * rows_b
    factor = fact[pl.ds(pl.multiple_of(first_y, rows_b), rows_b), :]
    groups_y = max(rows_b // 8, 8)
    low = lax.broadcasted_iota(jnp.int32, (8, lanes), 0).astype(f32)
    high_x = lax.broadcasted_iota(jnp.int32, (modes_x // 8, lanes), 0) * 8 - modes_x // 2
    high_y = lax.broadcasted_iota(jnp.int32, (groups_y, lanes), 0) * 8 + (first_y - modes_y // 2)
    high_x = high_x.astype(f32)
    high_y = high_y.astype(f32)

    def phases(position, high, rows):
        cos_l, sin_l = cos_sin(position * low)
        cos_h, sin_h = cos_sin(position * high)
        cosines, sines = [], []
        for m in range(rows // 8):
            c = jnp.broadcast_to(cos_h[m : m + 1], low.shape)
            s = jnp.broadcast_to(sin_h[m : m + 1], low.shape)
            cosines.append(c * cos_l - s * sin_l)
            sines.append(s * cos_l + c * sin_l)
        return jnp.concatenate(cosines, 0), jnp.concatenate(sines, 0)

    exchange_wait(0, recv_a)

    def project(with_tables, recv):
        def step(d, total):
            twisted = []
            for h in range(tiles):
                cols = slice(h * lanes, (h + 1) * lanes)
                if with_tables:
                    g = (d // size_w).astype(f32)
                    column = (lax.rem(d, size_w) * tiles + h).astype(f32)
                    off_x = recv[d, slots + 2 * h : slots + 2 * h + 1, :]
                    off_y = recv[d, slots + 2 * h + 1 : slots + 2 * h + 2, :]
                    px = (g + off_x) / count_x
                    py = (column + off_y) / count_y
                    cos_a, sin_a = phases(px, high_x, modes_x)
                    table_x[d, 0:modes_x, cols] = cos_a.astype(bf16)
                    table_x[d, modes_x : 2 * modes_x, cols] = sin_a.astype(bf16)
                    cos_b, sin_b = phases(py, high_y, rows_b)
                    cy = cos_b.astype(bf16).astype(f32)
                    sy = sin_b.astype(bf16).astype(f32)
                    cos_y[d, :, cols] = cy
                    sin_y[d, :, cols] = sy
                else:
                    cy = cos_y[d, :, cols]
                    sy = sin_y[d, :, cols]
                q_r = recv[d, h : h + 1, :]
                q_i = recv[d, tiles + h : tiles + h + 1, :]
                twisted.append(
                    jnp.concatenate([cy * q_r + sy * q_i, cy * q_i - sy * q_r], 0).astype(bf16)
                )
            return total + rows_dot(jnp.concatenate(twisted, 1), table_x[d])

        zero = jnp.zeros((2 * rows_b, 2 * modes_x), f32)
        return lax.fori_loop(0, devices, step, zero, unroll=unroll_project)

    def far_partial(total, slab, phase, target):
        top = total[:rows_b]
        low = total[rows_b:]
        real = top[:, :modes_x] + low[:, modes_x:]
        imag = low[:, :modes_x] - top[:, modes_x:]
        real = (real * factor).astype(bf16)
        imag = (imag * factor).astype(bf16)
        matrix = jnp.concatenate(
            [jnp.concatenate([real, -imag], 1), jnp.concatenate([imag, real], 1)], 0
        )

        def expand(d):
            summed = jnp.dot(matrix, table_x[d], preferred_element_type=f32)
            s_r = summed[:rows_b]
            s_i = summed[rows_b:]
            cy = cos_y[d]
            sy = sin_y[d]
            far_r = jnp.sum(s_r * cy - s_i * sy, 0, keepdims=True)
            far_i = jnp.sum(s_r * sy + s_i * cy, 0, keepdims=True)
            for h in range(tiles):
                cols = slice(h * lanes, (h + 1) * lanes)
                slab[d, h : h + 1, :] = far_r[:, cols]
                slab[d, tiles + h : tiles + h + 1, :] = far_i[:, cols]

        def step(k, carry):
            d = lax.rem(me + k, devices)
            expand(d)
            copy_to(phase, d, slab.at[d], target).start()
            return carry

        lax.fori_loop(1, devices, step, 0, unroll=unroll_expand)
        expand(me)

    def near_and_half(halo):
        for h in range(tiles):
            picked = []
            for j in range(9):
                slot = neighbor[0, h, j]
                row = slot // 3
                column = lax.rem(w * tiles + h + lax.rem(slot, 3) - 1 + count_y, count_y)
                picked.append(halo[row, column])
            left = jnp.concatenate(picked, 1)
            right = jnp.concatenate(
                [
                    jnp.concatenate([kernel_vmem[h, j, c] for j in range(9)], 0)
                    for c in range(2)
                ],
                1,
            )
            product = jnp.dot(left, right, preferred_element_type=f32)
            image[h, 0] = (
                0.5 * basis[h, 0] + product[:vectors, :lanes] - product[vectors:, lanes:]
            )
            image[h, 1] = (
                0.5 * basis[h, 1] + product[:vectors, lanes:] + product[vectors:, :lanes]
            )

    def far_of(recv, row):
        grouped = recv[:, row, :].reshape(vectors, shares, lanes)
        return jnp.sum(grouped, 1)

    def far_own(slab, recv):
        recv[me, 0:slots, :] = slab[me, 0:slots, :]

    far_partial(project(True, recv_a), send_f1, 1, recv_f1)
    far_own(send_f1, recv_f1)
    load.wait()
    for copy in copies_1:
        copy.wait_recv()
    near_and_half(halo_1)
    exchange_wait(1, recv_f1)

    inner_r = jnp.zeros((vectors, lanes), f32)
    inner_i = jnp.zeros((vectors, lanes), f32)
    for h in range(tiles):
        w_r = image[h, 0] + far_of(recv_f1, h)
        w_i = image[h, 1] + far_of(recv_f1, tiles + h)
        image[h, 0] = w_r
        image[h, 1] = w_i
        b_r = basis[h, 0]
        b_i = basis[h, 1]
        inner_r += b_r * w_r + b_i * w_i
        inner_i += b_r * w_i - b_i * w_r
    lane = lax.broadcasted_iota(jnp.int32, (vectors, lanes), 1)
    sums = [jnp.sum(x, 1, keepdims=True) for x in (square, inner_r, inner_i)]
    send_r[...] = jnp.where(lane == 0, sums[0], jnp.where(lane == 1, sums[1], sums[2]))
    exchange_start(2, lambda other: send_r, recv_r)
    recv_r[me] = send_r[...]
    exchange_wait(2, recv_r)
    sums = jnp.sum(recv_r[...], 0)
    scale = jnp.sqrt(sums[:, 0:1] / panels + eps_norm)
    inverse = 1.0 / scale
    inverse_2 = inverse * inverse
    coef_r = sums[:, 1:2] / panels * inverse_2
    coef_i = sums[:, 2:3] / panels * inverse_2

    square = jnp.zeros((vectors, lanes), f32)
    second = []
    for h in range(tiles):
        b_r = basis[h, 0]
        b_i = basis[h, 1]
        u_r = (image[h, 0] - (coef_r * b_r - coef_i * b_i)) * inverse
        u_i = (image[h, 1] - (coef_r * b_i + coef_i * b_r)) * inverse
        square += u_r * u_r + u_i * u_i
        second.append((u_r, u_i))
    stage(second, halo_2, send_b)
    copies_2 = halo_copies(1, halo_2)
    exchange_start(3, lambda other: send_b.at[other // shares], recv_b)
    for copy in copies_2:
        copy.start()
    recv_b[me] = send_b[my_vector]

    def put_square(d, carry):
        send_f2[d, slots : slots + vectors, :] = square
        return carry

    lax.fori_loop(0, devices, put_square, 0)
    exchange_wait(3, recv_b)
    far_partial(project(False, recv_b), send_f2, 4, recv_f2)
    recv_f2[me] = send_f2[me]
    for copy in copies_2:
        copy.wait_recv()
    near_and_half(halo_2)
    exchange_wait(4, recv_f2)
    update_sq = jnp.sum(recv_f2[:, slots : slots + vectors, :], 0)
    update_sq = jnp.sum(update_sq, 1, keepdims=True)
    update_scale = jnp.sqrt(update_sq / panels + eps_norm)
    inverse = 1.0 / update_scale
    for h in range(tiles):
        for c in range(2):
            image_out[h, c] = (image[h, c] + far_of(recv_f2, c * tiles + h)) * inverse
    row = lax.broadcasted_iota(jnp.int32, (vectors, lanes), 0)
    for number, value in enumerate((scale, coef_r, coef_i, update_scale)):
        line = jnp.sum(jnp.where(row == lane, value, 0.0), 0, keepdims=True)
        arnoldi_out[number : number + 1, :] = line[:, :vectors]

    for copy in copies_1 + copies_2:
        copy.wait_send()
    for phase, target in enumerate((recv_a, recv_f1, recv_r, recv_b, recv_f2)):
        sent_wait(phase, target)


def hand_over(image, arnoldi, image_out, arnoldi_out):
    image_out[...] = image[...]
    arnoldi_out[...] = arnoldi[...]


def per_device(
    size_t,
    size_w,
    residual,
    kernel,
    offsets,
    neighbor,
    frequency,
    lattice_x,
    lattice_y,
    spectral_weight,
):
    strips, tiles, _, vectors, lanes = residual.shape
    modes_x, modes_y = spectral_weight.shape[1:]
    devices = size_t * size_w
    assert strips == 1 and lanes == 128 and size_w == 2 and size_t > 2
    assert devices % vectors == 0
    rows_b = modes_y // (devices // vectors)
    slots = 2 * tiles
    vmem = pl.BlockSpec(memory_space=pltpu.VMEM)
    smem = pl.BlockSpec(memory_space=pltpu.SMEM)
    halo = pltpu.VMEM((3, size_w * tiles, 2 * vectors, lanes), bf16)
    image, arnoldi = pl.pallas_call(
        functools.partial(body, size_t, size_w, tiles, vectors, modes_x, modes_y),
        out_shape=(
            jax.ShapeDtypeStruct((tiles, 2, vectors, lanes), f32),
            jax.ShapeDtypeStruct((4, vectors), f32),
        ),
        in_specs=[
            vmem,
            pl.BlockSpec(memory_space=pl.ANY),
            vmem,
            smem,
            smem,
            vmem,
            vmem,
            vmem,
        ],
        out_specs=(vmem, vmem),
        scratch_shapes=[
            pltpu.VMEM((vectors, 2 * slots, lanes), f32),
            pltpu.VMEM((devices, 2 * slots, lanes), f32),
            pltpu.VMEM((devices, slots, lanes), f32),
            pltpu.VMEM((devices, slots, lanes), f32),
            pltpu.VMEM((vectors, lanes), f32),
            pltpu.VMEM((devices, vectors, lanes), f32),
            pltpu.VMEM((vectors, slots, lanes), f32),
            pltpu.VMEM((devices, slots, lanes), f32),
            pltpu.VMEM((devices, slots + vectors, lanes), f32),
            pltpu.VMEM((devices, slots + vectors, lanes), f32),
            halo,
            halo,
            pltpu.VMEM((devices, 2 * modes_x, tiles * lanes), bf16),
            pltpu.VMEM((devices, rows_b, tiles * lanes), f32),
            pltpu.VMEM((devices, rows_b, tiles * lanes), f32),
            pltpu.VMEM((modes_y, modes_x), f32),
            pltpu.VMEM((tiles, 2, vectors, lanes), f32),
            pltpu.VMEM((tiles, 2, vectors, lanes), f32),
            pltpu.VMEM((tiles, 9, 2, lanes, lanes), bf16),
            pltpu.SemaphoreType.DMA,
            pltpu.SemaphoreType.DMA((5,)),
            pltpu.SemaphoreType.DMA((5,)),
            pltpu.SemaphoreType.DMA((2, 5)),
            pltpu.SemaphoreType.DMA((2, 5)),
        ],
        compiler_params=pltpu.CompilerParams(
            collective_id=0, has_side_effects=True, vmem_limit_bytes=56 * 1024 * 1024
        ),
        name="arnoldi_pair",
    )(
        residual[0],
        kernel[0],
        offsets[0],
        neighbor,
        frequency,
        lattice_x[None],
        lattice_y[None],
        spectral_weight,
    )
    image, arnoldi = pl.pallas_call(
        hand_over,
        out_shape=(
            jax.ShapeDtypeStruct(image.shape, f32),
            jax.ShapeDtypeStruct(arnoldi.shape, f32),
        ),
        in_specs=[vmem, vmem],
        out_specs=(vmem, vmem),
        name="hand_over",
    )(image, arnoldi)
    return image[None], arnoldi


def solution(mesh):
    return jax.shard_map(
        functools.partial(per_device, mesh.shape["tile"], mesh.shape["wave"]),
        mesh=mesh,
        in_specs=(
            P(("grp", "tile"), "wave", None, None, None),
            P(("grp", "tile"), "wave", None, None, None, None),
            P(("grp", "tile"), "wave", None, None),
            P(("grp", "tile"), "wave", None),
            P("grp"),
            P(),
            P(),
            P(),
        ),
        out_specs=(P(("grp", "tile"), "wave", None, None, None), P("grp", None)),
        check_vma=False,
    )
```
